256 devices in a mesh: sta: 4 (over x), clu: 64 (over z, y, core).
Axes of the slice: x: 4, y: 4, z: 8, core: 2. Of those that a mesh axis runs over, the one named last changes fastest.
Arguments:
- spectra: bfloat16 [2048, 256, 128], P('clu', 'sta'), may hold values from -6 to 6
- partials: bfloat16 [2048, 4, 256], P('clu', None, 'sta')
- pair_list: int32 [2048, 50], P('clu'), may hold values from -1 to 103, as said below
- station_mask: int32 [2048, 50, 256], P('clu', None, 'sta'), may hold values 0 or 1
- exports: int32 [384, 12], P('clu'), may hold values from 0 to 31
Outputs:
- normal_blocks: float32 [16, 51, 2048], P('sta', None, 'clu')
- right_sides: float32 [4, 2048], P('sta', 'clu')
The draws below stay inside these ranges and needn't reach their ends.
Inputs may be any that keep to these rules, and one draw needn't show every extreme that they name: `pair_list`: each event's valid entries come first and the rest are -1; every event has 25 to 50 valid entries and the first event of every cluster has all 50. A valid entry below 32 names an event of the same cluster; entry 32 + h * 12 + c names the c-th event sent to this cluster by the cluster at cycle offset -o(h) from it, o(h) as for exports.
All inputs are finite; a program needn't handle non-finite values. No bound on the sum of `station_mask` on one device may be relied on, other than what follows from the above.
Results may differ from the reference program's by a relative error of at most 0.0047.
Values may be sent and summed in bfloat16 or wider, within the bound.
A program may use at most 64 MiB of HBM per device.

```python
import math
import jax
import jax.numpy as jnp
from jax import lax

F = 64
NB = 50
HALF = 3
CAP = 12
E_DEV = 32
EVENTS = 2048
STATIONS = 256
CANDS = 104
N_CLU = 64


def draw_partials(key, part):
    station_part = jax.random.normal(jax.random.fold_in(key, 11), (1, 4, STATIONS), jnp.float32)
    own_part = jax.random.normal(jax.random.fold_in(key, 12), (EVENTS, 4, STATIONS), jnp.float32)
    return (station_part + 0.6 * own_part).astype(jnp.bfloat16)


def draw_pair_list(key, part):
    counts = jax.random.randint(jax.random.fold_in(key, 21), (EVENTS,), NB // 2, NB + 1)
    firsts = jnp.arange(EVENTS, dtype=jnp.int32) % E_DEV == 0
    counts = jnp.where(firsts, NB, counts)
    near_pick = jax.random.randint(jax.random.fold_in(key, 22), (EVENTS, NB), 0, E_DEV)
    far_pick = jax.random.randint(jax.random.fold_in(key, 23), (EVENTS, NB), E_DEV, CANDS)
    coin = jax.random.randint(jax.random.fold_in(key, 24), (EVENTS, NB), 0, 5)
    chosen = jnp.where(coin < 3, near_pick, far_pick)
    slot_ids = jnp.arange(NB, dtype=jnp.int32)[None, :]
    return jnp.where(slot_ids < counts[:, None], chosen, -1).astype(jnp.int32)


def plant(array, own_key, least, high):
    place = [jax.random.randint(jax.random.fold_in(own_key, axis), (), 0, length) for axis, length in enumerate(array.shape)]
    longest = array.shape.index(max(array.shape))
    neighbour = place[:longest] + [(place[longest] + 1) % array.shape[longest]] + place[longest + 1:]
    return array.at[tuple(place)].set(least).at[tuple(neighbour)].set(high)


def level_of(stream_key, extent, pieces, smallest, high):
    gain = 1.0
    for dim, parts in pieces:
        steps = jax.random.uniform(jax.random.fold_in(jax.random.fold_in(stream_key, 6), dim), (parts,), jnp.float32, smallest / len(pieces), high / len(pieces))
        gain = gain * jnp.repeat(jnp.exp(steps), extent[dim] // parts).reshape((-1,) + (1,) * (len(extent) - 1 - dim))
    return gain


def scatter_about(key, extent, spread, most, pieces=(), held_as=jnp.bfloat16):
    entries = spread * jax.random.normal(key, extent, jnp.float32)
    if pieces:
        entries = entries * level_of(key, extent, pieces, -0.22, 0.18)
    return jnp.clip(entries, -most, most).astype(held_as)


def setup_inputs(seed: int = 0) -> dict:
    streams_of = jax.random.split(jax.random.key(seed), 6)
    spectra = scatter_about(streams_of[0], (EVENTS, STATIONS, 2 * F), 1.0, 6.0, ((0, 64), (1, 4)))
    partials = draw_partials(jax.random.fold_in(streams_of[5], 71), 0)
    pair_list = draw_pair_list(jax.random.fold_in(streams_of[5], 71), 0)
    station_mask = plant((jax.random.randint(streams_of[3], (EVENTS, NB, STATIONS), 0, 4) < 3).astype(jnp.int32), jax.random.fold_in(streams_of[3], 1), 0, 1)
    exports = plant(jax.random.randint(streams_of[4], (N_CLU * 2 * HALF, CAP), 0, E_DEV), jax.random.fold_in(streams_of[4], 1), 0, E_DEV - 1).astype(jnp.int32)
    return {"spectra": spectra, "partials": partials, "pair_list": pair_list, "station_mask": station_mask, "exports": exports}


def lag_tables(freq_count):
    freq_values = jnp.arange(freq_count, dtype=jnp.float32) * (math.pi / freq_count)
    lag_values = jnp.arange(2 * freq_count - 1, dtype=jnp.float32) - (freq_count - 1)
    phase_grid = freq_values[:, None] * lag_values[None, :]
    cosine_grid = jnp.cos(phase_grid)
    sine_grid = jnp.sin(phase_grid)
    real_rows = jnp.concatenate([cosine_grid, -freq_values[:, None] * sine_grid], axis=1)
    imag_rows = jnp.concatenate([-sine_grid, -freq_values[:, None] * cosine_grid], axis=1)
    lag_table = jnp.concatenate([real_rows, imag_rows], axis=0).astype(jnp.bfloat16)
    return (lag_table, lag_values)

def pair_weights(spec_one, spec_two, energy_one, energy_two, lag_table, lag_values, freq_count):
    first_vals = spec_one.astype(jnp.float32)
    second_vals = spec_two.astype(jnp.float32)
    real_a = first_vals[..., :freq_count]
    imag_a = first_vals[..., freq_count:]
    real_b = second_vals[..., :freq_count]
    imag_b = second_vals[..., freq_count:]
    cross_spec = jnp.concatenate([real_a * real_b + imag_a * imag_b, imag_a * real_b - real_a * imag_b], axis=-1).astype(jnp.bfloat16)
    lead_shape = cross_spec.shape[:-1]
    lagged = jnp.dot(cross_spec.reshape(-1, 2 * freq_count), lag_table, preferred_element_type=jnp.float32)
    lag_count = lag_values.shape[0]
    inverse = lax.rsqrt((energy_one * energy_two).reshape(-1) + 1e-06)
    correlation = lagged[:, :lag_count] * inverse[:, None]
    slope_fn = lagged[:, lag_count:] * inverse[:, None]
    power_sum = lax.optimization_barrier(jnp.sum(correlation * correlation, axis=1))
    rough_sum = lax.optimization_barrier(jnp.sum(slope_fn * slope_fn, axis=1))
    delay_lag = lax.optimization_barrier(jnp.sum(correlation * correlation * lag_values[None, :], axis=1)) / (power_sum + 1e-06)
    weight = power_sum / (power_sum + 0.125 * rough_sum + 1e-06)
    return (weight.reshape(lead_shape), delay_lag.reshape(lead_shape))

def reference(spectra, partials, pair_list, station_mask, exports):
    highest = lax.Precision.HIGHEST
    lag_table, lag_values = lag_tables(F)
    energy = lax.optimization_barrier(jnp.sum(jnp.square(spectra.astype(jnp.float32)), axis=-1))
    event_ids = jnp.arange(EVENTS, dtype=jnp.int32)
    owner_ids = (event_ids // E_DEV)[:, None]
    clipped = jnp.maximum(pair_list, 0)
    local_ids = owner_ids * E_DEV + jnp.minimum(clipped, E_DEV - 1)
    far_slot = jnp.maximum(clipped - E_DEV, 0)
    slot_group = far_slot // CAP
    cycle_offset = slot_group - HALF + (slot_group >= HALF).astype(jnp.int32)
    source = jnp.mod(owner_ids - cycle_offset + N_CLU, N_CLU)
    far_ids = source * E_DEV + exports[source * (2 * HALF) + slot_group, far_slot % CAP]
    partner = jnp.where(clipped < E_DEV, local_ids, far_ids).astype(jnp.int32)
    live_pairs = (pair_list >= 0).astype(jnp.float32)[..., None] * station_mask.astype(jnp.float32)
    block_size = max(E_DEV // 16, 1)
    group_count = EVENTS // block_size

    def one_block(inputs):
        spec_a, geo_a, energy_a, partner_b, live_b = inputs
        weight, delay_lag = pair_weights(spec_a[:, None], spectra[partner_b], energy_a[:, None], energy[partner_b], lag_table, lag_values, F)
        scaled = weight * live_b / STATIONS
        geo_one = geo_a.astype(jnp.float32)
        geo_two = partials[partner_b].astype(jnp.float32)
        diag_one = jnp.einsum('rks,ris,rjs->ijr', scaled, geo_one, geo_one, precision=highest).reshape(16, -1)
        off_diag = -jnp.einsum('rks,ris,rkjs->ijkr', scaled, geo_one, geo_two, precision=highest).reshape(16, NB, -1)
        right_one = jnp.einsum('rks,ris->ir', scaled * delay_lag, geo_one, precision=highest)
        diag_two = jnp.einsum('rks,rkis,rkjs->rkij', scaled, geo_two, geo_two, precision=highest).reshape(-1, 16)
        right_two = -jnp.einsum('rks,rkis->rki', scaled * delay_lag, geo_two, precision=highest).reshape(-1, 4)
        return (diag_one, off_diag, right_one, diag_two, right_two)
    blocked = (spectra.reshape(group_count, block_size, STATIONS, 2 * F), partials.reshape(group_count, block_size, 4, STATIONS), energy.reshape(group_count, block_size, STATIONS), partner.reshape(group_count, block_size, NB), live_pairs.reshape(group_count, block_size, NB, STATIONS))
    diag_one, off_diag, right_one, diag_two, right_two = lax.map(one_block, blocked)
    targets = partner.reshape(-1)
    diagonal = diag_one.transpose(1, 0, 2).reshape(16, EVENTS)
    diagonal = diagonal + jax.ops.segment_sum(diag_two.reshape(EVENTS * NB, 16), targets, num_segments=EVENTS).T
    off_blocks = off_diag.transpose(1, 2, 0, 3).reshape(16, NB, EVENTS)
    right_hand = right_one.transpose(1, 0, 2).reshape(4, EVENTS)
    right_hand = right_hand + jax.ops.segment_sum(right_two.reshape(EVENTS * NB, 4), targets, num_segments=EVENTS).T
    normal_blocks = jnp.concatenate([diagonal[:, None, :], off_blocks], axis=1)
    return (normal_blocks, right_hand)
```

```python
import functools
import math

import jax
import jax.numpy as jnp
import numpy as np
from jax import lax
from jax.experimental import pallas as pl
from jax.experimental.pallas import tpu as pltpu
from jax.sharding import PartitionSpec as P

F32 = jnp.float32
BF16 = jnp.bfloat16
NT = (((1,), (1,)), ((), ()))
GROUP = 4
PAD_K = 16
MESH = pl.DeviceIdType.MESH


def moment_tables(freq_count):
    n = 2 * freq_count
    f = np.arange(freq_count, dtype=np.float32) * np.float32(math.pi / freq_count)
    lags = np.arange(n - 1, dtype=np.float32) - (freq_count - 1)
    phase = f[:, None] * lags[None, :]
    cosine = np.cos(phase).astype(BF16).astype(np.float64)
    sine = np.sin(phase).astype(BF16).astype(np.float64)
    moment = -2.0 * np.einsum("l,fl,gl->fg", lags.astype(np.float64), cosine, sine)
    w = np.arange(freq_count) * (math.pi / freq_count)
    sign = 1.0 - 2.0 * (np.arange(freq_count) % 2)
    rough = freq_count / 8.0 * w * w
    rough_high = rough.astype(np.float32).astype(BF16).astype(np.float64)
    one = np.zeros((2 * n, 2 * n))
    two = np.zeros((2 * n, n))
    for h in range(2):
        part = slice(h * freq_count, (h + 1) * freq_count)
        later = slice(n + h * freq_count, n + (h + 1) * freq_count)
        one[part, part] = moment
        one[part, n + 4 + h] = sign
        one[h * freq_count, n + 8 + h] = 1.0
        one[later, n + 6 + h] = sign * w
        one[n + h * freq_count, n + 10 + h] = 1.0
        two[part, 0 + h] = freq_count
        two[part, 2 + h] = rough_high
        two[part, 14 + h] = rough - rough_high
        two[later, 12 + h] = 1.0
    ones = np.zeros((16, n))
    ones[0, :freq_count] = 1.0
    ones[1, freq_count:] = 1.0
    order = np.zeros((n, n))
    for k in range(PAD_K * GROUP):
        order[k, (k % GROUP) * PAD_K + k // GROUP] = 1.0
        order[k, n // 2 + (k % GROUP) * PAD_K + k // GROUP] = 1.0
    return [x.astype(np.float32).astype(BF16) for x in (one, two, ones, order)]


def kernel(
    offsets, shape,
    exports_ref, pairs_ref, spec_ref, geo_in_ref, pairs_v_ref, exports_v_ref, mask_ref,
    table_ref, sums_ref, ones_ref, order_ref,
    off_out, side_out,
    spec_send, spec_got, geo_send, geo_got,
    br_ref, bi_ref, bq_ref, en_ref, geo_ref, slot_ref, rbuf, gbuf, off_ref, acc_ref, own_ref,
    side_ref, off_got, side_got,
    spec_ss, spec_rs, geo_ss, geo_rs, off_ss, off_rs, side_ss, side_rs,
):
    events, neighbours, sta_n, clu_n, all_stations = shape
    groups_out = len(offsets)
    capacity = spec_send.shape[1]
    imported = groups_out * capacity
    cands = events + imported
    rows = br_ref.shape[0]
    groups = -(-neighbours // GROUP)
    me_s, me_c = lax.axis_index("sta"), lax.axis_index("clu")
    sta_at = [lax.rem(me_s + d, sta_n) for d in range(sta_n)]
    clu_to = [lax.rem(me_c + o + clu_n, clu_n) for o in offsets] + [me_c]
    clu_back = [lax.rem(me_c - o + clu_n, clu_n) for o in offsets] + [me_c]
    peers = [(d, h) for d in range(sta_n) for h in range(groups_out + 1) if d > 0 or h < groups_out]

    barrier = pltpu.get_barrier_semaphore()
    for d, h in peers:
        pl.semaphore_signal(barrier, inc=1, device_id=(sta_at[d], clu_to[h]), device_id_type=MESH)

    lane8 = lax.broadcasted_iota(jnp.int32, (8, 128), 1) // 32

    def spread_geo(i, c):
        tile = geo_in_ref[i].astype(F32)
        tile = jnp.concatenate([tile, jnp.zeros_like(tile)], axis=1)
        tile = jnp.concatenate([tile, pltpu.roll(tile, 96, 1)], axis=0)
        tile = jnp.where(lane8 == 0, tile, 0.0)
        tile = tile + pltpu.roll(tile, 32, 1)
        geo_ref[i] = tile + pltpu.roll(tile, 64, 1)
        return c

    lax.fori_loop(0, events, spread_geo, 0, unroll=4)

    for h in range(groups_out):
        for c in range(capacity):
            e = exports_ref[h, c]
            spec_send[h, c] = spec_ref[e]
            geo_send[h, c] = geo_ref[e].astype(BF16)

    pl.semaphore_wait(barrier, len(peers))

    def halo(h):
        target = (me_s, clu_to[h])
        return (
            pltpu.make_async_remote_copy(
                src_ref=spec_send.at[h], dst_ref=spec_got.at[h], send_sem=spec_ss.at[h], recv_sem=spec_rs.at[h],
                device_id=target, device_id_type=MESH,
            ),
            pltpu.make_async_remote_copy(
                src_ref=geo_send.at[h], dst_ref=geo_got.at[h], send_sem=geo_ss.at[h], recv_sem=geo_rs.at[h],
                device_id=target, device_id_type=MESH,
            ),
        )

    halos = [copy for h in range(groups_out) for copy in halo(h)]
    for copy in halos:
        copy.start()

    half = 32
    low = lax.broadcasted_iota(jnp.int32, (half, 128), 1) < 64
    ones_rows = ones_ref[...]

    def prepare(tiles, base):
        stacked = []
        for u, tile in enumerate(tiles):
            tile = tile.astype(F32)
            top, bottom = tile[:half], tile[half:]
            real = jnp.where(low, top, pltpu.roll(bottom, 64, 1))
            imag = jnp.where(low, pltpu.roll(top, 64, 1), bottom)
            power = real * real + imag * imag
            br_ref[base + u] = real
            bi_ref[base + u] = imag
            bq_ref[base + u] = power
            stacked.append(power.astype(BF16))
        energy = lax.dot_general(ones_rows, jnp.concatenate(stacked, axis=0), NT, preferred_element_type=F32)[0:8]
        for u in range(GROUP):
            one = jnp.where(lane8 == u, energy, 0.0)
            one = one + pltpu.roll(one, 32, 1)
            en_ref[base + u] = one + pltpu.roll(one, 64, 1)

    def prepare_own(i, c):
        prepare([spec_ref[i * GROUP + u] for u in range(GROUP)], i * GROUP)
        return c

    lax.fori_loop(0, events // GROUP, prepare_own, 0)
    zero_tile = jnp.zeros((half, 128), F32)
    for r in range(cands, rows):
        br_ref[r] = zero_tile
        bi_ref[r] = zero_tile
        bq_ref[r] = zero_tile
        en_ref[r] = jnp.zeros((8, 128), F32)
        geo_ref[r] = jnp.zeros((8, 128), F32)

    rbuf[...] = jnp.zeros_like(rbuf)
    gbuf[...] = jnp.zeros_like(gbuf)
    acc_ref[...] = jnp.zeros_like(acc_ref)
    off_ref[...] = jnp.zeros_like(off_ref)

    pairs_v = pairs_v_ref[...].astype(F32) + 1.0
    pairs_v = jnp.concatenate([pairs_v, jnp.zeros((events, 128 - neighbours), F32)], axis=1).astype(BF16)
    slot_ref[...] = jnp.dot(pairs_v, order_ref[...], preferred_element_type=F32) - 1.0

    lane16 = lax.broadcasted_iota(jnp.int32, (16, 128), 1) // 32
    block_mask = [jnp.where(lane16 == u, 1.0, 0.0).astype(BF16) for u in range(GROUP)]
    cand_iota = lax.broadcasted_iota(jnp.int32, (cands, 128), 0).astype(F32)
    row_e = lax.broadcasted_iota(jnp.int32, (128, 128), 0) // 32 * 32
    col_e = lax.broadcasted_iota(jnp.int32, (128, 128), 1)
    table = table_ref[...]
    sums = sums_ref[...]

    def pick4(parts, lanes):
        return jnp.where(
            lanes < 2, jnp.where(lanes == 0, parts[0], parts[1]), jnp.where(lanes == 2, parts[2], parts[3])
        )

    for copy in halos:
        copy.wait()

    def prepare_got(h):
        for i in range(capacity // GROUP):
            base = events + h * capacity + i * GROUP
            prepare([spec_got[h, i * GROUP + u] for u in range(GROUP)], base)
            for u in range(GROUP):
                geo_ref[base + u] = geo_got[h, i * GROUP + u].astype(F32)

    def prepare_step(h, c):
        prepare_got(h)
        return c

    lax.fori_loop(0, groups_out, prepare_step, 0)

    def one_event(e, carry):
        ar, ai, aq = br_ref[e], bi_ref[e], bq_ref[e]
        ids = []
        for k in range(groups * GROUP):
            if k < neighbours:
                c = pairs_ref[e, k]
                ids.append(jnp.where(c < 0, cands, c))
            else:
                ids.append(cands)
        xr_all, xi_all, q_all = [], [], []
        for c in ids:
            br, bi = br_ref[c], bi_ref[c]
            xr_all.append((ar * br + ai * bi).astype(BF16))
            xi_all.append((ai * br - ar * bi).astype(BF16))
            q_all.append((aq * bq_ref[c]).astype(BF16))
        xr = jnp.concatenate(xr_all, axis=0)
        xi = jnp.concatenate(xi_all, axis=0)
        q = jnp.concatenate(q_all, axis=0)
        y = jnp.dot(jnp.concatenate([xr, xi], axis=1), table, preferred_element_type=F32)
        z = (y[:, :128] * xi.astype(F32)).astype(BF16)
        t = jnp.dot(jnp.concatenate([q, z], axis=1), sums, preferred_element_type=F32) + y[:, 128:]
        for kg in range(groups):
            four = ids[kg * GROUP : (kg + 1) * GROUP]
            rbuf[pl.ds(kg * 16, 16), :] = t[kg * 128 : (kg + 1) * 128].T[:16]
            gbuf[pl.ds(kg * 16, 8), :] = pick4([geo_ref[c] for c in four], lane8)
            gbuf[pl.ds(kg * 16 + 8, 8), :] = pick4([en_ref[c] for c in four], lane8)

        masks = []
        for u in range(GROUP):
            count = len(range(u, neighbours, GROUP))
            part = mask_ref[e, pl.ds(u, count, stride=GROUP), :].astype(F32) * (1.0 / all_stations)
            part = jnp.concatenate([part, jnp.zeros((PAD_K - count, part.shape[1]), F32)], axis=0)
            masks.append(jnp.concatenate([part, jnp.zeros_like(part)], axis=1))
        live = []
        for h in range(2):
            parts = []
            for u in range(GROUP):
                shift = (32 * u - 32 * h) % 128
                parts.append(pltpu.roll(masks[u], shift, 1) if shift else masks[u])
            live.append(pick4(parts, lane16))

        def quantity(ref, r):
            return ref[pl.ds(r, PAD_K, stride=16), :]

        ga = geo_ref[e]
        ea = en_ref[e]
        weighted, moved, offs = [], [], [None] * 16
        for h in range(2):
            first = quantity(rbuf, 8 + h)
            first_i = quantity(rbuf, 10 + h)
            alt = quantity(rbuf, 4 + h)
            alt_i = quantity(rbuf, 6 + h)
            power = quantity(rbuf, h) + 64.0 * (first * first - first_i * first_i) - alt * alt
            rough8 = quantity(rbuf, 2 + h) + quantity(rbuf, 14 + h) - 0.125 * (alt_i * alt_i)
            small = 1e-6 * (ea[h : h + 1] * quantity(gbuf, 8 + h) + 1e-6)
            weight = live[h] * power / (power + rough8 + small)
            delayed = weight * quantity(rbuf, 12 + h) / (power + small)
            weighted.append(weight)
            moved.append(delayed)
            gb = [quantity(gbuf, 4 * h + j) for j in range(4)]
            for i in range(4):
                wi = weight * ga[4 * h + i : 4 * h + i + 1]
                for j in range(4):
                    term = wi * gb[j]
                    offs[4 * i + j] = term if h == 0 else offs[4 * i + j] + term
        place = jnp.where(col_e == row_e + e, -1.0, 0.0).astype(BF16)
        offs = jnp.concatenate(offs, axis=0)
        off_ref[...] += jnp.dot(offs.astype(BF16), place, preferred_element_type=F32)

        columns = []
        for n, value in enumerate(weighted + moved):
            own_ref[n, pl.ds(e, 1), :] = jnp.sum(value, axis=0, keepdims=True)
            value_high = value.astype(BF16)
            value_low = (value - value_high.astype(F32)).astype(BF16)
            columns.append(
                jnp.concatenate([v * m for v in (value_high, value_low) for m in block_mask], axis=0)
            )
        columns = jnp.concatenate(columns, axis=1)
        hot = jnp.where(cand_iota == slot_ref[pl.ds(e, 1), :], 1.0, 0.0).astype(BF16)
        acc_ref[...] += jnp.dot(hot, columns, preferred_element_type=F32)
        return carry

    lax.fori_loop(0, events, one_event, 0)

    share = off_ref.shape[0] // sta_n

    def off_copy(d):
        return pltpu.make_async_remote_copy(
            src_ref=off_ref.at[pl.ds(sta_at[d] * share, share)], dst_ref=off_got.at[d - 1],
            send_sem=off_ss.at[d - 1], recv_sem=off_rs.at[d - 1],
            device_id=(sta_at[d], me_c), device_id_type=MESH,
        )

    off_copies = [off_copy(d) for d in range(1, sta_n)]
    for copy in off_copies:
        copy.start()

    lane_out = lax.broadcasted_iota(jnp.int32, (cands, 128), 1)
    pad = jnp.zeros((imported, 128), F32)
    totals = []
    for n in range(4):
        own = jnp.concatenate([own_ref[n], pad], axis=0)
        part = acc_ref[:, n * 128 : (n + 1) * 128]
        totals.append(part + own if n < 2 else own - part)

    result = jnp.zeros((cands, 128), F32)
    geo_t = geo_ref.reshape(rows * 8, 128)
    geos = [geo_t[pl.ds(n, cands, stride=8), :] for n in range(8)]
    for i in range(4):
        scaled = [totals[h] * geos[4 * h + i] for h in range(2)]
        for j in range(i, 4):
            value = jnp.sum(scaled[0] * geos[j] + scaled[1] * geos[4 + j], axis=1, keepdims=True)
            keep = (lane_out == 8 * i + j) | (lane_out == 8 * j + i)
            result = jnp.where(keep, value, result)
        value = jnp.sum(totals[2] * geos[i] + totals[3] * geos[4 + i], axis=1, keepdims=True)
        result = jnp.where(lane_out == 8 * i + 4, value, result)
    result = jnp.concatenate([result, jnp.zeros((128 - cands, 128), F32)], axis=0).T
    for x in range(sta_n):
        side_ref[x] = result[8 * x : 8 * x + 8]

    def side_copy(n):
        d, h = peers[n]
        return pltpu.make_async_remote_copy(
            src_ref=side_ref.at[sta_at[d]], dst_ref=side_got.at[n],
            send_sem=side_ss.at[n], recv_sem=side_rs.at[n],
            device_id=(sta_at[d], clu_back[h]), device_id_type=MESH,
        )

    side_copies = [side_copy(n) for n in range(len(peers))]
    for copy in side_copies:
        copy.start()
    for copy in off_copies:
        copy.wait()
    total = off_ref[pl.ds(me_s * share, share), :]
    for d in range(1, sta_n):
        total = total + off_got[d - 1]
    off_out[...] = total
    for copy in side_copies:
        copy.wait()

    kept = side_ref[me_s]
    for n, (d, h) in enumerate(peers):
        if h == groups_out:
            kept = kept + side_got[n]
    lane_c = lax.broadcasted_iota(jnp.int32, (8, 128), 1)
    away = jnp.zeros((8, 128), F32)
    for h in range(groups_out):
        part = jnp.zeros((8, 128), F32)
        for n, (d, g) in enumerate(peers):
            if g == h:
                part = part + side_got[n]
        lowest = events + h * capacity
        away = jnp.where((lane_c >= lowest) & (lane_c < lowest + capacity), part, away)
    owner = jnp.where(
        lax.broadcasted_iota(jnp.int32, (events, 128), 0) == exports_v_ref[...], 1.0, 0.0
    ).astype(BF16)
    back = jnp.zeros((8, events), F32)
    for _ in range(3):
        piece = away.astype(BF16)
        back = back + lax.dot_general(piece, owner, NT, preferred_element_type=F32)
        away = away - piece.astype(F32)
    side_out[...] = kept[:, :events] + back


def on_device(spectra, partials, pair_list, station_mask, exports):
    events, stations, two_freq = spectra.shape
    sta_n, clu_n = lax.axis_size("sta"), lax.axis_size("clu")
    groups_out, capacity = exports.shape
    half_span = groups_out // 2
    neighbours = pair_list.shape[1]
    imported = groups_out * capacity
    cands = events + imported
    rows = cands + 1
    offsets = [h - half_span + (1 if h >= half_span else 0) for h in range(groups_out)]
    n_peers = sta_n * (groups_out + 1) - 1
    exports_v = jnp.pad(exports.reshape(1, -1), ((0, 0), (events, 128 - cands)), constant_values=-1)
    smem = pl.BlockSpec(memory_space=pltpu.SMEM)
    vmem = pl.BlockSpec(memory_space=pltpu.VMEM)
    dma = pltpu.SemaphoreType.DMA
    share = 16 * PAD_K // sta_n
    off, side = pl.pallas_call(
        functools.partial(kernel, offsets, (events, neighbours, sta_n, clu_n, stations * sta_n)),
        out_shape=(jax.ShapeDtypeStruct((share, 128), F32), jax.ShapeDtypeStruct((8, events), F32)),
        in_specs=[smem, smem] + [vmem] * 9,
        out_specs=(vmem, vmem),
        scratch_shapes=[
            pltpu.VMEM((groups_out, capacity, stations, two_freq), BF16),
            pltpu.VMEM((groups_out, capacity, stations, two_freq), BF16),
            pltpu.VMEM((groups_out, capacity, 8, 128), BF16),
            pltpu.VMEM((groups_out, capacity, 8, 128), BF16),
            pltpu.VMEM((rows, 32, 128), F32),
            pltpu.VMEM((rows, 32, 128), F32),
            pltpu.VMEM((rows, 32, 128), F32),
            pltpu.VMEM((rows, 8, 128), F32),
            pltpu.VMEM((rows, 8, 128), F32),
            pltpu.VMEM((events, 128), F32),
            pltpu.VMEM((PAD_K * 16, 128), F32),
            pltpu.VMEM((PAD_K * 16, 128), F32),
            pltpu.VMEM((16 * PAD_K, 128), F32),
            pltpu.VMEM((cands, 512), F32),
            pltpu.VMEM((4, events, 128), F32),
            pltpu.VMEM((sta_n, 8, 128), F32),
            pltpu.VMEM((sta_n - 1, share, 128), F32),
            pltpu.VMEM((n_peers, 8, 128), F32),
            dma((groups_out,)), dma((groups_out,)), dma((groups_out,)), dma((groups_out,)),
            dma((sta_n - 1,)), dma((sta_n - 1,)), dma((n_peers,)), dma((n_peers,)),
        ],
        compiler_params=pltpu.CompilerParams(
            vmem_limit_bytes=48 << 20, collective_id=0, has_side_effects=True
        ),
    )(
        exports, pair_list, spectra, partials, pair_list, exports_v, station_mask,
        *[jnp.asarray(x) for x in moment_tables(two_freq // 2)],
    )
    off = off.reshape(16 // sta_n, PAD_K * GROUP, events)[:, :neighbours]
    normal = jnp.concatenate([side[: 16 // sta_n, None, :], off], axis=1)
    return (normal, side[4:5])


def solution(mesh):
    return jax.shard_map(
        on_device,
        mesh=mesh,
        in_specs=(
            P("clu", "sta", None),
            P("clu", None, "sta"),
            P("clu", None),
            P("clu", None, "sta"),
            P("clu", None),
        ),
        out_specs=(P("sta", None, "clu"), P("sta", "clu")),
        check_vma=False,
    )
```

```python
import functools
import math

import jax
import jax.numpy as jnp
import numpy as np
from jax import lax
from jax.experimental import pallas as pl
from jax.experimental.pallas import tpu as pltpu
from jax.sharding import PartitionSpec as P

F32 = jnp.float32
BF16 = jnp.bfloat16
NT = (((1,), (1,)), ((), ()))
CHUNKS = 2
GROUP = 8
PAD_K = 8
REP = 16
MESH = pl.DeviceIdType.MESH


def moment_tables(freq_count):
    n = 2 * freq_count
    f = np.arange(freq_count, dtype=np.float32) * np.float32(math.pi / freq_count)
    lags = np.arange(n - 1, dtype=np.float32) - (freq_count - 1)
    phase = f[:, None] * lags[None, :]
    cosine = np.cos(phase).astype(BF16).astype(np.float64)
    sine = np.sin(phase).astype(BF16).astype(np.float64)
    moment = -2.0 * np.einsum("l,fl,gl->fg", lags.astype(np.float64), cosine, sine)
    w = np.arange(freq_count) * (math.pi / freq_count)
    sign = 1.0 - 2.0 * (np.arange(freq_count) % 2)
    rough = freq_count / 8.0 * w * w
    rough_high = rough.astype(np.float32).astype(BF16).astype(np.float64)
    one = np.zeros((2 * n, 2 * n))
    two = np.zeros((2 * n, n))
    for h in range(2):
        part = slice(h * freq_count, (h + 1) * freq_count)
        later = slice(n + h * freq_count, n + (h + 1) * freq_count)
        one[part, part] = moment
        one[part, n + 4 + h] = sign
        one[h * freq_count, n + 8 + h] = 1.0
        one[later, n + 6 + h] = sign * w
        one[n + h * freq_count, n + 10 + h] = 1.0
        two[part, 0 + h] = freq_count
        two[part, 2 + h] = rough_high
        two[part, 14 + h] = rough - rough_high
        two[later, 12 + h] = 1.0
    ones = np.zeros((16, n))
    ones[0, :freq_count] = 1.0
    ones[1, freq_count:] = 1.0
    order = np.zeros((n, n))
    for k in range(PAD_K * GROUP):
        order[k, (k % GROUP) * PAD_K + k // GROUP] = 1.0
        order[k, GROUP * PAD_K + (k % GROUP) * PAD_K + k // GROUP] = 1.0
    both = np.zeros((2 * n, 5 * n))
    both[:, : 2 * n] = one
    both[:, 2 * n : 3 * n] = two
    both[:n, 3 * n : 4 * n] = order
    both[:16, 4 * n :] = ones
    return both.astype(np.float32).astype(BF16)


def kernel(
    offsets, shape,
    exports_ref, pairs_ref, spec_hbm, geo_hbm, pairs_hbm, exports_hbm, mask_hbm, consts_hbm,
    off_out, right_out,
    spec_ref, geo_in_ref, pairs_v_ref, exports_v_ref, mask_ref, consts_ref, exports_row, load_sems,
    spec_send, spec_got, geo_send, geo_got,
    br_ref, bi_ref, bq_ref, en_ref, geo_ref, slot_ref, off_ref, acc_ref, own_ref,
    side_ref, off_got, side_got, last_ref,
    cross_a, cross_b, quad_a, quad_b, rbuf_a, rbuf_b, gbuf_a, gbuf_b, live_ref, hot_ref, place_ref,
    spec_ss, spec_rs, geo_ss, geo_rs, off_ss, off_rs, side_ss, side_rs,
):
    events, neighbours, sta_n, clu_n, all_stations = shape
    groups_out = len(offsets)
    capacity = geo_send.shape[1]
    imported = groups_out * capacity
    cands = events + imported
    rows = geo_ref.shape[0]
    me_s, me_c = lax.axis_index("sta"), lax.axis_index("clu")
    sta_at = [lax.rem(me_s + d, sta_n) for d in range(sta_n)]
    clu_to = [lax.rem(me_c + o + clu_n, clu_n) for o in offsets] + [me_c]
    clu_back = [lax.rem(me_c - o + clu_n, clu_n) for o in offsets] + [me_c]
    peers = [(d, h) for d in range(sta_n) for h in range(groups_out + 1) if d > 0 or h < groups_out]

    loads = [
        pltpu.make_async_copy(source, target, load_sems.at[n])
        for n, (source, target) in enumerate((
            (spec_hbm, spec_ref), (geo_hbm, geo_in_ref), (consts_hbm, consts_ref), (exports_hbm, exports_v_ref),
            (pairs_hbm, pairs_v_ref), (mask_hbm, mask_ref),
        ))
    ]
    for copy in loads:
        copy.start()
    barrier = pltpu.get_barrier_semaphore()
    for d, h in peers:
        pl.semaphore_signal(barrier, inc=1, device_id=(sta_at[d], clu_to[h]), device_id_type=MESH)

    loads[0].wait()
    loads[1].wait()
    for h in range(groups_out):
        for c in range(capacity):
            e = exports_ref[h, c]
            tile = spec_ref[e]
            for ch in range(CHUNKS):
                spec_send[ch, h, c] = jnp.concatenate(
                    [tile[REP * ch : REP * (ch + 1)], tile[32 + REP * ch : 32 + REP * (ch + 1)]], axis=0
                )
            geo_send[h, c] = geo_in_ref[e]

    pl.semaphore_wait(barrier, len(peers))

    def halo(ch, h):
        return pltpu.make_async_remote_copy(
            src_ref=spec_send.at[ch, h], dst_ref=spec_got.at[ch, h],
            send_sem=spec_ss.at[ch, h], recv_sem=spec_rs.at[ch, h],
            device_id=(me_s, clu_to[h]), device_id_type=MESH,
        )

    def geo_halo(h):
        return pltpu.make_async_remote_copy(
            src_ref=geo_send.at[h], dst_ref=geo_got.at[h], send_sem=geo_ss.at[h], recv_sem=geo_rs.at[h],
            device_id=(me_s, clu_to[h]), device_id_type=MESH,
        )

    order_h = sorted(range(groups_out), key=lambda h: -abs(offsets[h]))
    geo_halos = [geo_halo(h) for h in order_h]
    halos = [[halo(ch, h) for h in order_h] for ch in range(CHUNKS)]
    for copy in geo_halos + sum(halos, []):
        copy.start()

    block8 = lax.broadcasted_iota(jnp.int32, (8, 128), 1) // REP
    lane8 = lax.broadcasted_iota(jnp.int32, (8, 128), 1)
    low = lax.broadcasted_iota(jnp.int32, (REP, 128), 1) < 64
    for copy in loads[2:]:
        copy.wait()
    ones_rows = consts_ref[0:16, 512:640]

    def repeat(tile):
        tile = tile + pltpu.roll(tile, 16, 1)
        tile = tile + pltpu.roll(tile, 32, 1)
        return tile + pltpu.roll(tile, 64, 1)

    def spread_geo(tile, c):
        tile = tile.astype(F32)
        tile = jnp.concatenate([tile, jnp.zeros_like(tile)], axis=1)
        for ch in range(CHUNKS):
            first = pltpu.roll(tile, 128 - REP * ch, 1) if ch else tile
            both = jnp.concatenate([first, pltpu.roll(tile, 128 - 32 - REP * ch, 1)], axis=0)
            geo_ref[c, 8 * ch : 8 * ch + 8] = repeat(jnp.where(block8 == 0, both, 0.0))

    def prepare(ch, tiles, base):
        stacked = []
        for u, (top, bottom) in enumerate(tiles):
            top, bottom = top.astype(F32), bottom.astype(F32)
            real = jnp.where(low, top, pltpu.roll(bottom, 64, 1))
            imag = jnp.where(low, pltpu.roll(top, 64, 1), bottom)
            power = real * real + imag * imag
            br_ref[ch, base + u] = real
            bi_ref[ch, base + u] = imag
            bq_ref[ch, base + u] = power
            stacked.append(power)
        stacked = jnp.concatenate(stacked, axis=0).astype(BF16)
        energy = lax.dot_general(ones_rows, stacked, NT, preferred_element_type=F32)[0:8]
        for u in range(GROUP):
            en_ref[ch, base + u] = repeat(jnp.where(block8 == u, energy, 0.0))

    def prepare_own(i, c):
        for ch in range(CHUNKS):
            tiles = []
            for u in range(GROUP):
                tile = spec_ref[i * GROUP + u]
                tiles.append((tile[REP * ch : REP * (ch + 1)], tile[32 + REP * ch : 32 + REP * (ch + 1)]))
            prepare(ch, tiles, i * GROUP)
        for u in range(GROUP):
            spread_geo(geo_in_ref[i * GROUP + u], i * GROUP + u)
        return c

    lax.fori_loop(0, events // GROUP, prepare_own, 0)
    for r in range(cands, rows):
        for ch in range(CHUNKS):
            br_ref[ch, r] = jnp.zeros((REP, 128), F32)
            bi_ref[ch, r] = jnp.zeros((REP, 128), F32)
            bq_ref[ch, r] = jnp.zeros((REP, 128), F32)
            en_ref[ch, r] = jnp.zeros((8, 128), F32)
        geo_ref[r] = jnp.zeros((8 * CHUNKS, 128), F32)

    for ref in (acc_ref, off_ref, rbuf_a, rbuf_b, gbuf_a, gbuf_b, last_ref):
        ref[...] = jnp.zeros_like(ref)

    exports_row[...] = jnp.full_like(exports_row, -1)
    exports_row[0:groups_out, 0:capacity] = exports_v_ref[...]
    pairs_v = pairs_v_ref[...].astype(F32) + 1.0
    pairs_v = jnp.concatenate([pairs_v, jnp.zeros((events, 128 - neighbours), F32)], axis=1).astype(BF16)
    slot_ref[...] = jnp.dot(pairs_v, consts_ref[0:128, 384:512], preferred_element_type=F32) - 1.0

    cand_iota = lax.broadcasted_iota(jnp.int32, (cands, 128), 0).astype(F32)
    row_e = lax.broadcasted_iota(jnp.int32, (128, 256), 0) // REP * 32
    col_e = lax.broadcasted_iota(jnp.int32, (128, 256), 1)
    table = consts_ref[:, 0:256]
    sums = consts_ref[:, 256:384]

    def pick(parts, base=0):
        if len(parts) == 1:
            return parts[0]
        mid = len(parts) // 2
        return jnp.where(block8 < base + mid, pick(parts[:mid], base), pick(parts[mid:], base + mid))

    def slot_ids(e):
        ids = []
        for k in range(neighbours):
            c = pairs_ref[e, k]
            ids.append(jnp.where(c < 0, cands, c))
        return ids

    def stage_a(ch, pair, cross, quad):
        for v in range(2):
            e = 2 * pair + v
            ar, ai, aq = br_ref[ch, e], bi_ref[ch, e], bq_ref[ch, e]
            for k, c in enumerate(slot_ids(e)):
                br, bi = br_ref[ch, c], bi_ref[ch, c]
                at = pl.ds((v * neighbours + k) * REP, REP)
                cross[at, 0:128] = (ar * br + ai * bi).astype(BF16)
                cross[at, 128:256] = (ai * br - ar * bi).astype(BF16)
                quad[at, :] = (aq * bq_ref[ch, c]).astype(BF16)

    def stage_b(ch, pair, cross, quad, rbuf, gbuf):
        y = jnp.dot(cross[...], table, preferred_element_type=F32)
        z = (y[:, :128] * cross[:, 128:256].astype(F32)).astype(BF16)
        t = jnp.dot(jnp.concatenate([quad[...], z], axis=1), sums, preferred_element_type=F32) + y[:, 128:]
        for v in range(2):
            ids = slot_ids(2 * pair + v)
            for kg in range(-(-neighbours // GROUP)):
                first = v * neighbours * REP + kg * 128
                last = min(first + 128, (v + 1) * neighbours * REP)
                part = t[first:last]
                if part.shape[0] < 128:
                    part = jnp.concatenate([part, jnp.zeros((128 - part.shape[0], 128), F32)], axis=0)
                rbuf[v, pl.ds(kg * 16, 16), :] = part.T[:16]
                some = ids[kg * GROUP : (kg + 1) * GROUP]
                some = some + [cands] * (GROUP - len(some))
                gbuf[v, pl.ds(kg * 16, 8), :] = pick([geo_ref[c, 8 * ch : 8 * ch + 8] for c in some])
                gbuf[v, pl.ds(kg * 16 + 8, 8), :] = pick([en_ref[ch, c] for c in some])

    def make_live(e):
        masks = []
        for u in range(GROUP):
            count = len(range(u, neighbours, GROUP))
            part = mask_ref[pl.ds(u * events + e, count, stride=GROUP * events), :].astype(F32)
            part = jnp.concatenate([part, jnp.zeros((PAD_K - count, part.shape[1]), F32)], axis=0)
            masks.append(jnp.concatenate([part, jnp.zeros_like(part)], axis=1))
        for ch in range(CHUNKS):
            for h in range(2):
                parts = []
                for u in range(GROUP):
                    shift = (REP * u - 32 * h - REP * ch) % 128
                    parts.append(pltpu.roll(masks[u], shift, 1) if shift else masks[u])
                live_ref[ch, e, 8 * h : 8 * h + 8] = pick(parts) * (1.0 / all_stations)

    def make_pair(pair, c):
        lanes = lax.broadcasted_iota(jnp.int32, (1, 128), 1)
        slots = jnp.where(lanes < 64, slot_ref[pl.ds(2 * pair, 1), :], slot_ref[pl.ds(2 * pair + 1, 1), :])
        hot_ref[pair] = jnp.where(cand_iota == slots, 1.0, 0.0).astype(BF16)
        for v in range(2):
            make_live(2 * pair + v)
            place = jnp.where(col_e == row_e + (2 * pair + v), -1.0, 0.0).astype(BF16)
            place_ref[pair, 128 * v : 128 * v + 128] = place
        return c

    lax.fori_loop(0, events // 2, make_pair, 0)

    def stage_c(ch, pair, rbuf, gbuf):
        offs_pair, column_pair = [], []
        for v in range(2):
            e = 2 * pair + v

            def quantity(ref, r, v=v):
                return ref[v, pl.ds(r, PAD_K, stride=16), :]

            live = live_ref[ch, e]
            ga = geo_ref[e, 8 * ch : 8 * ch + 8]
            ea = en_ref[ch, e]
            weighted, moved, offs = [], [], [None] * 16
            for h in range(2):
                first = quantity(rbuf, 8 + h)
                first_i = quantity(rbuf, 10 + h)
                alt = quantity(rbuf, 4 + h)
                alt_i = quantity(rbuf, 6 + h)
                power = quantity(rbuf, h) + 64.0 * (first * first - first_i * first_i) - alt * alt
                rough8 = quantity(rbuf, 2 + h) + quantity(rbuf, 14 + h) - 0.125 * (alt_i * alt_i)
                small = 1e-6 * (ea[h : h + 1] * quantity(gbuf, 8 + h) + 1e-6)
                weight = live[8 * h : 8 * h + 8] * power / (power + rough8 + small)
                delayed = weight * quantity(rbuf, 12 + h) / (power + small)
                weighted.append(weight)
                moved.append(delayed)
                gb = [quantity(gbuf, 4 * h + j) for j in range(4)]
                for i in range(4):
                    wi = weight * ga[4 * h + i : 4 * h + i + 1]
                    for j in range(4):
                        term = wi * gb[j]
                        offs[4 * i + j] = term if h == 0 else offs[4 * i + j] + term
            offs_pair.append(jnp.concatenate(offs, axis=0))
            columns = []
            for n, value in enumerate(weighted + moved):
                own_ref[ch, n, pl.ds(e, 1), :] = jnp.sum(value, axis=0, keepdims=True)
                columns.append(
                    jnp.concatenate([jnp.where(block8 == u, value, 0.0) for u in range(GROUP)], axis=0)
                )
            column_pair.append(jnp.concatenate(columns, axis=1))
        offs = jnp.concatenate(offs_pair, axis=1).astype(BF16)
        off_ref[...] += jnp.dot(offs, place_ref[pair], preferred_element_type=F32)
        columns = jnp.concatenate(column_pair, axis=0).astype(BF16)
        acc_ref[ch] += jnp.dot(hot_ref[pair], columns, preferred_element_type=F32)

    for copy in geo_halos:
        copy.wait()

    def spread_got(h, c):
        for i in range(capacity):
            spread_geo(geo_got[h, i], events + h * capacity + i)
        return c

    lax.fori_loop(0, groups_out, spread_got, 0)

    for ch in range(CHUNKS):
        for copy in halos[ch]:
            copy.wait()

        for part in range(imported // GROUP):
            tiles = []
            for n in range(part * GROUP, (part + 1) * GROUP):
                tile = spec_got[ch, n // capacity, n % capacity]
                tiles.append((tile[:REP], tile[REP:]))
            prepare(ch, tiles, events + part * GROUP)

        if ch:
            rbuf_b[...] = jnp.zeros_like(rbuf_b)
        stage_a(ch, 0, cross_a, quad_a)
        pairs = events // 2

        def two_pairs(i, c, ch=ch):
            p = 2 * i
            stage_a(ch, p + 1, cross_b, quad_b)
            stage_b(ch, p, cross_a, quad_a, rbuf_a, gbuf_a)
            stage_c(ch, jnp.maximum(p - 1, 0), rbuf_b, gbuf_b)
            stage_a(ch, jnp.minimum(p + 2, pairs - 1), cross_a, quad_a)
            stage_b(ch, p + 1, cross_b, quad_b, rbuf_b, gbuf_b)
            stage_c(ch, p, rbuf_a, gbuf_a)
            return c

        lax.fori_loop(0, pairs // 2, two_pairs, 0)
        stage_c(ch, pairs - 1, rbuf_b, gbuf_b)

    share = off_ref.shape[0] // sta_n

    def off_copy(d):
        return pltpu.make_async_remote_copy(
            src_ref=off_ref.at[pl.ds(sta_at[d] * share, share)], dst_ref=off_got.at[d - 1],
            send_sem=off_ss.at[d - 1], recv_sem=off_rs.at[d - 1],
            device_id=(sta_at[d], me_c), device_id_type=MESH,
        )

    off_copies = [off_copy(d) for d in range(1, sta_n)]
    for copy in off_copies:
        copy.start()

    lane_out = lax.broadcasted_iota(jnp.int32, (cands, 128), 1)
    pad = jnp.zeros((imported, 128), F32)
    geo_t = geo_ref.reshape(rows * 8 * CHUNKS, 128)
    partial_sums = [None] * 20
    for ch in range(CHUNKS):
        totals = []
        for n in range(4):
            own = jnp.concatenate([own_ref[ch, n], pad], axis=0)
            part = acc_ref[ch, :, n * 128 : (n + 1) * 128]
            totals.append(part + own if n < 2 else own - part)
        geos = [geo_t[pl.ds(8 * ch + n, cands, stride=8 * CHUNKS), :] for n in range(8)]
        for i in range(4):
            scaled = [totals[h] * geos[4 * h + i] for h in range(2)]
            for j in range(i, 5):
                if j < 4:
                    term = scaled[0] * geos[j] + scaled[1] * geos[4 + j]
                else:
                    term = totals[2] * geos[i] + totals[3] * geos[4 + i]
                n = 5 * i + j
                partial_sums[n] = term if ch == 0 else partial_sums[n] + term
    result = jnp.zeros((cands, 128), F32)
    for i in range(4):
        for j in range(i, 5):
            value = jnp.sum(partial_sums[5 * i + j], axis=1, keepdims=True)
            keep = lane_out == 8 * i + j
            if j < 4:
                keep = keep | (lane_out == 8 * j + i)
            result = jnp.where(keep, value, result)
    result = jnp.concatenate([result, jnp.zeros((128 - cands, 128), F32)], axis=0).T
    for x in range(sta_n):
        side_ref[x] = result[8 * x : 8 * x + 8]

    def side_copy(n):
        d, h = peers[n]
        return pltpu.make_async_remote_copy(
            src_ref=side_ref.at[sta_at[d]], dst_ref=side_got.at[n],
            send_sem=side_ss.at[n], recv_sem=side_rs.at[n],
            device_id=(sta_at[d], clu_back[h]), device_id_type=MESH,
        )

    side_copies = [side_copy(n) for n in range(len(peers))]
    for copy in side_copies:
        copy.start()
    for copy in off_copies:
        copy.wait()
    total = off_ref[pl.ds(pl.multiple_of(me_s * share, share), share), :]
    for d in range(1, sta_n):
        total = total + off_got[d - 1]
    for ij in range(share // PAD_K):
        for u in range(GROUP):
            count = len(range(u, neighbours, GROUP))
            block = total[ij * PAD_K : ij * PAD_K + PAD_K, u * 32 : u * 32 + 32]
            last_ref[pl.ds(ij * 128 + 1 + u, count, stride=GROUP), 0:32] = block[:count]
    for copy in side_copies:
        copy.wait()

    kept = side_ref[me_s]
    for n, (d, h) in enumerate(peers):
        if h == groups_out:
            kept = kept + side_got[n]
    away = jnp.zeros((8, 128), F32)
    for h in range(groups_out):
        part = jnp.zeros((8, 128), F32)
        for n, (d, g) in enumerate(peers):
            if g == h:
                part = part + side_got[n]
        lowest = events + h * capacity
        away = jnp.where((lane8 >= lowest) & (lane8 < lowest + capacity), part, away)
    owner_row = jnp.full((1, 128), -1, jnp.int32)
    for h in range(groups_out):
        lowest = events + h * capacity
        inside = (lane8[0:1] >= lowest) & (lane8[0:1] < lowest + capacity)
        owner_row = jnp.where(inside, pltpu.roll(exports_row[h : h + 1, :], lowest, 1), owner_row)
    owner = jnp.where(
        lax.broadcasted_iota(jnp.int32, (events, 128), 0) == owner_row, 1.0, 0.0
    ).astype(BF16)
    back = jnp.zeros((8, events), F32)
    for _ in range(3):
        piece = away.astype(BF16)
        back = back + lax.dot_general(piece, owner, NT, preferred_element_type=F32)
        away = away - piece.astype(F32)
    side = kept[:, :events] + back
    right_out[...] = side[4:5]
    for ij in range(share // PAD_K):
        last_ref[ij * 128 : ij * 128 + 1, 0:32] = side[ij : ij + 1]
        off_out[ij] = last_ref[ij * 128 : ij * 128 + 128, :].T[:events, : neighbours + 1]


def on_device(spectra, partials, pair_list, station_mask, exports):
    events, stations, two_freq = spectra.shape
    sta_n, clu_n = lax.axis_size("sta"), lax.axis_size("clu")
    groups_out, capacity = exports.shape
    half_span = groups_out // 2
    neighbours = pair_list.shape[1]
    imported = groups_out * capacity
    cands = events + imported
    rows = cands + 1
    offsets = [h - half_span + (1 if h >= half_span else 0) for h in range(groups_out)]
    n_peers = sta_n * (groups_out + 1) - 1
    masks = station_mask.transpose(1, 0, 2).reshape(neighbours * events, stations)
    smem = pl.BlockSpec(memory_space=pltpu.SMEM)
    vmem = pl.BlockSpec(memory_space=pltpu.VMEM)
    dma = pltpu.SemaphoreType.DMA
    share = 16 * PAD_K // sta_n
    off, right = pl.pallas_call(
        functools.partial(kernel, offsets, (events, neighbours, sta_n, clu_n, stations * sta_n)),
        out_shape=(
            jax.ShapeDtypeStruct((16 // sta_n, events, neighbours + 1), F32),
            jax.ShapeDtypeStruct((1, events), F32),
        ),
        in_specs=[smem, smem] + [pl.BlockSpec(memory_space=pl.ANY)] * 6,
        out_specs=(vmem, vmem),
        scratch_shapes=[
            pltpu.VMEM(spectra.shape, BF16),
            pltpu.VMEM(partials.shape, BF16),
            pltpu.VMEM(pair_list.shape, jnp.int32),
            pltpu.VMEM(exports.shape, jnp.int32),
            pltpu.VMEM(masks.shape, jnp.int32),
            pltpu.VMEM((2 * two_freq, 5 * two_freq), BF16),
            pltpu.VMEM((8, 128), jnp.int32),
            dma((6,)),
            pltpu.VMEM((CHUNKS, groups_out, capacity, 2 * REP, two_freq), BF16),
            pltpu.VMEM((CHUNKS, groups_out, capacity, 2 * REP, two_freq), BF16),
            pltpu.VMEM((groups_out, capacity, 4, stations), BF16),
            pltpu.VMEM((groups_out, capacity, 4, stations), BF16),
            pltpu.VMEM((CHUNKS, rows, REP, 128), F32),
            pltpu.VMEM((CHUNKS, rows, REP, 128), F32),
            pltpu.VMEM((CHUNKS, rows, REP, 128), F32),
            pltpu.VMEM((CHUNKS, rows, 8, 128), F32),
            pltpu.VMEM((rows, 8 * CHUNKS, 128), F32),
            pltpu.VMEM((events, 128), F32),
            pltpu.VMEM((16 * PAD_K, 256), F32),
            pltpu.VMEM((CHUNKS, cands, 512), F32),
            pltpu.VMEM((CHUNKS, 4, events, 128), F32),
            pltpu.VMEM((sta_n, 8, 128), F32),
            pltpu.VMEM((sta_n - 1, share, 256), F32),
            pltpu.VMEM((n_peers, 8, 128), F32),
            pltpu.VMEM((16 // sta_n * 128, 128), F32),
            pltpu.VMEM((2 * neighbours * REP, 256), BF16),
            pltpu.VMEM((2 * neighbours * REP, 256), BF16),
            pltpu.VMEM((2 * neighbours * REP, 128), BF16),
            pltpu.VMEM((2 * neighbours * REP, 128), BF16),
            pltpu.VMEM((2, PAD_K * 16, 128), F32),
            pltpu.VMEM((2, PAD_K * 16, 128), F32),
            pltpu.VMEM((2, PAD_K * 16, 128), F32),
            pltpu.VMEM((2, PAD_K * 16, 128), F32),
            pltpu.VMEM((CHUNKS, events, 16, 128), F32),
            pltpu.VMEM((events // 2, cands, 128), BF16),
            pltpu.VMEM((events // 2, 256, 256), BF16),
            dma((CHUNKS, groups_out)), dma((CHUNKS, groups_out)), dma((groups_out,)), dma((groups_out,)),
            dma((sta_n - 1,)), dma((sta_n - 1,)), dma((n_peers,)), dma((n_peers,)),
        ],
        compiler_params=pltpu.CompilerParams(
            vmem_limit_bytes=60 << 20, collective_id=0, has_side_effects=True
        ),
    )(
        exports, pair_list, spectra, partials, pair_list, exports, masks,
        jnp.asarray(moment_tables(two_freq // 2)),
    )
    return (off.transpose(0, 2, 1), right)


def solution(mesh):
    return jax.shard_map(
        on_device,
        mesh=mesh,
        in_specs=(
            P("clu", "sta", None),
            P("clu", None, "sta"),
            P("clu", None),
            P("clu", None, "sta"),
            P("clu", None),
        ),
        out_specs=(P("sta", None, "clu"), P("sta", "clu")),
        check_vma=False,
    )
```

```python
import functools
import math

import jax
import jax.numpy as jnp
import numpy as np
from jax import lax
from jax.experimental import pallas as pl
from jax.experimental.pallas import tpu as pltpu
from jax.sharding import PartitionSpec as P

F32 = jnp.float32
BF16 = jnp.bfloat16
NT = (((1,), (1,)), ((), ()))
CHUNKS = 2
GROUP = 8
PAD_K = 8
REP = 16
MESH = pl.DeviceIdType.MESH


def moment_tables(freq_count):
    n = 2 * freq_count
    f = np.arange(freq_count, dtype=np.float32) * np.float32(math.pi / freq_count)
    lags = np.arange(n - 1, dtype=np.float32) - (freq_count - 1)
    phase = f[:, None] * lags[None, :]
    cosine = np.cos(phase).astype(BF16).astype(np.float64)
    sine = np.sin(phase).astype(BF16).astype(np.float64)
    moment = -2.0 * np.einsum("l,fl,gl->fg", lags.astype(np.float64), cosine, sine)
    w = np.arange(freq_count) * (math.pi / freq_count)
    sign = 1.0 - 2.0 * (np.arange(freq_count) % 2)
    rough = freq_count / 8.0 * w * w
    rough_high = rough.astype(np.float32).astype(BF16).astype(np.float64)
    one = np.zeros((2 * n, 2 * n))
    two = np.zeros((2 * n, n))
    for h in range(2):
        part = slice(h * freq_count, (h + 1) * freq_count)
        later = slice(n + h * freq_count, n + (h + 1) * freq_count)
        one[part, part] = moment
        one[part, n + 4 + h] = sign
        one[h * freq_count, n + 8 + h] = 1.0
        one[later, n + 6 + h] = sign * w
        one[n + h * freq_count, n + 10 + h] = 1.0
        two[part, 0 + h] = freq_count
        two[part, 2 + h] = rough_high
        two[part, 14 + h] = rough - rough_high
        two[later, 12 + h] = 1.0
    ones = np.zeros((16, n))
    ones[0, :freq_count] = 1.0
    ones[1, freq_count:] = 1.0
    order = np.zeros((n, n))
    for k in range(PAD_K * GROUP):
        order[k, (k % GROUP) * PAD_K + k // GROUP] = 1.0
        order[k, GROUP * PAD_K + (k % GROUP) * PAD_K + k // GROUP] = 1.0
    both = np.zeros((2 * n, 5 * n))
    both[:, : 2 * n] = one
    both[:, 2 * n : 3 * n] = two
    both[:n, 3 * n : 4 * n] = order
    both[:16, 4 * n :] = ones
    return both.astype(np.float32).astype(BF16)


def kernel(
    offsets, shape,
    exports_ref, pairs_ref, spec_hbm, geo_hbm, pairs_hbm, exports_hbm, mask_hbm, consts_hbm,
    off_out, right_out,
    spec_ref, geo_in_ref, pairs_v_ref, exports_v_ref, mask_ref, consts_ref, exports_row, load_sems,
    spec_send, spec_got, geo_send, geo_got,
    br_ref, bi_ref, bq_ref, en_ref, geo_ref, slot_ref, off_ref, acc_ref, own_ref,
    side_ref, off_got, side_got, last_ref,
    cross_a, cross_b, quad_a, quad_b, rbuf_a, rbuf_b, gbuf_a, gbuf_b, live_ref, hot_ref, place_ref,
    spec_ss, spec_rs, geo_ss, geo_rs, off_ss, off_rs, side_ss, side_rs,
):
    events, neighbours, sta_n, clu_n, all_stations = shape
    groups_out = len(offsets)
    capacity = geo_send.shape[1]
    imported = groups_out * capacity
    cands = events + imported
    rows = geo_ref.shape[0]
    me_s, me_c = lax.axis_index("sta"), lax.axis_index("clu")
    sta_at = [lax.rem(me_s + d, sta_n) for d in range(sta_n)]
    clu_to = [lax.rem(me_c + o + clu_n, clu_n) for o in offsets] + [me_c]
    clu_back = [lax.rem(me_c - o + clu_n, clu_n) for o in offsets] + [me_c]
    peers = [(d, h) for d in range(sta_n) for h in range(groups_out + 1) if d > 0 or h < groups_out]

    loads = [
        pltpu.make_async_copy(source, target, load_sems.at[n])
        for n, (source, target) in enumerate((
            (spec_hbm, spec_ref), (geo_hbm, geo_in_ref), (consts_hbm, consts_ref), (exports_hbm, exports_v_ref),
            (pairs_hbm, pairs_v_ref), (mask_hbm, mask_ref),
        ))
    ]
    for copy in loads:
        copy.start()
    barrier = pltpu.get_barrier_semaphore()
    for d, h in peers:
        pl.semaphore_signal(barrier, inc=1, device_id=(sta_at[d], clu_to[h]), device_id_type=MESH)

    loads[0].wait()
    loads[1].wait()
    for h in range(groups_out):
        for c in range(capacity):
            e = exports_ref[h, c]
            tile = spec_ref[e]
            for ch in range(CHUNKS):
                spec_send[ch, h, c] = jnp.concatenate(
                    [tile[REP * ch : REP * (ch + 1)], tile[32 + REP * ch : 32 + REP * (ch + 1)]], axis=0
                )
            geo_send[h, c] = geo_in_ref[e]

    pl.semaphore_wait(barrier, len(peers))

    def halo(ch, h):
        return pltpu.make_async_remote_copy(
            src_ref=spec_send.at[ch, h], dst_ref=spec_got.at[ch, h],
            send_sem=spec_ss.at[ch, h], recv_sem=spec_rs.at[ch, h],
            device_id=(me_s, clu_to[h]), device_id_type=MESH,
        )

    def geo_halo(h):
        return pltpu.make_async_remote_copy(
            src_ref=geo_send.at[h], dst_ref=geo_got.at[h], send_sem=geo_ss.at[h], recv_sem=geo_rs.at[h],
            device_id=(me_s, clu_to[h]), device_id_type=MESH,
        )

    order_h = sorted(range(groups_out), key=lambda h: -abs(offsets[h]))
    geo_halos = [geo_halo(h) for h in order_h]
    halos = [[halo(ch, h) for h in order_h] for ch in range(CHUNKS)]
    for copy in geo_halos + halos[0]:
        copy.start()

    block8 = lax.broadcasted_iota(jnp.int32, (8, 128), 1) // REP
    lane8 = lax.broadcasted_iota(jnp.int32, (8, 128), 1)
    low = lax.broadcasted_iota(jnp.int32, (REP, 128), 1) < 64
    for copy in loads[2:]:
        copy.wait()
    ones_rows = consts_ref[0:16, 512:640]

    def repeat(tile):
        tile = tile + pltpu.roll(tile, 16, 1)
        tile = tile + pltpu.roll(tile, 32, 1)
        return tile + pltpu.roll(tile, 64, 1)

    def spread_geo(tile, c):
        tile = tile.astype(F32)
        tile = jnp.concatenate([tile, jnp.zeros_like(tile)], axis=1)
        for ch in range(CHUNKS):
            first = pltpu.roll(tile, 128 - REP * ch, 1) if ch else tile
            both = jnp.concatenate([first, pltpu.roll(tile, 128 - 32 - REP * ch, 1)], axis=0)
            geo_ref[c, 8 * ch : 8 * ch + 8] = repeat(jnp.where(block8 == 0, both, 0.0))

    def prepare(ch, tiles, base):
        stacked = []
        for u, (top, bottom) in enumerate(tiles):
            top, bottom = top.astype(F32), bottom.astype(F32)
            real = jnp.where(low, top, pltpu.roll(bottom, 64, 1))
            imag = jnp.where(low, pltpu.roll(top, 64, 1), bottom)
            power = real * real + imag * imag
            br_ref[ch, base + u] = real
            bi_ref[ch, base + u] = imag
            bq_ref[ch, base + u] = power
            stacked.append(power)
        stacked = jnp.concatenate(stacked, axis=0).astype(BF16)
        energy = lax.dot_general(ones_rows, stacked, NT, preferred_element_type=F32)[0:8]
        for u in range(GROUP):
            en_ref[ch, base + u] = repeat(jnp.where(block8 == u, energy, 0.0))

    def prepare_own(i, c):
        for ch in range(CHUNKS):
            tiles = []
            for u in range(GROUP):
                tile = spec_ref[i * GROUP + u]
                tiles.append((tile[REP * ch : REP * (ch + 1)], tile[32 + REP * ch : 32 + REP * (ch + 1)]))
            prepare(ch, tiles, i * GROUP)
        for u in range(GROUP):
            spread_geo(geo_in_ref[i * GROUP + u], i * GROUP + u)
        return c

    lax.fori_loop(0, events // GROUP, prepare_own, 0)
    for r in range(cands, rows):
        for ch in range(CHUNKS):
            br_ref[ch, r] = jnp.zeros((REP, 128), F32)
            bi_ref[ch, r] = jnp.zeros((REP, 128), F32)
            bq_ref[ch, r] = jnp.zeros((REP, 128), F32)
            en_ref[ch, r] = jnp.zeros((8, 128), F32)
        geo_ref[r] = jnp.zeros((8 * CHUNKS, 128), F32)

    for ref in (acc_ref, off_ref, rbuf_a, rbuf_b, gbuf_a, gbuf_b, last_ref):
        ref[...] = jnp.zeros_like(ref)

    exports_row[...] = jnp.full_like(exports_row, -1)
    exports_row[0:groups_out, 0:capacity] = exports_v_ref[...]
    pairs_v = pairs_v_ref[...].astype(F32) + 1.0
    pairs_v = jnp.concatenate([pairs_v, jnp.zeros((events, 128 - neighbours), F32)], axis=1).astype(BF16)
    slot_ref[...] = jnp.dot(pairs_v, consts_ref[0:128, 384:512], preferred_element_type=F32) - 1.0

    cand_iota = lax.broadcasted_iota(jnp.int32, (cands, 128), 0).astype(F32)
    row_e = lax.broadcasted_iota(jnp.int32, (128, 256), 0) // REP * 32
    col_e = lax.broadcasted_iota(jnp.int32, (128, 256), 1)
    table = consts_ref[:, 0:256]
    sums = consts_ref[:, 256:384]

    def pick(parts, base=0):
        if len(parts) == 1:
            return parts[0]
        mid = len(parts) // 2
        return jnp.where(block8 < base + mid, pick(parts[:mid], base), pick(parts[mid:], base + mid))

    def slot_ids(e):
        ids = []
        for k in range(neighbours):
            c = pairs_ref[e, k]
            ids.append(jnp.where(c < 0, cands, c))
        return ids

    def stage_a(ch, pair, cross, quad):
        for v in range(2):
            e = 2 * pair + v
            ar, ai, aq = br_ref[ch, e], bi_ref[ch, e], bq_ref[ch, e]
            for k, c in enumerate(slot_ids(e)):
                br, bi = br_ref[ch, c], bi_ref[ch, c]
                at = pl.ds((v * neighbours + k) * REP, REP)
                cross[at, 0:128] = (ar * br + ai * bi).astype(BF16)
                cross[at, 128:256] = (ai * br - ar * bi).astype(BF16)
                quad[at, :] = (aq * bq_ref[ch, c]).astype(BF16)

    def stage_b(ch, pair, cross, quad, rbuf, gbuf):
        y = jnp.dot(cross[...], table, preferred_element_type=F32)
        z = (y[:, :128] * cross[:, 128:256].astype(F32)).astype(BF16)
        t = jnp.dot(jnp.concatenate([quad[...], z], axis=1), sums, preferred_element_type=F32) + y[:, 128:]
        for v in range(2):
            ids = slot_ids(2 * pair + v)
            for kg in range(-(-neighbours // GROUP)):
                first = v * neighbours * REP + kg * 128
                last = min(first + 128, (v + 1) * neighbours * REP)
                part = t[first:last]
                if part.shape[0] < 128:
                    part = jnp.concatenate([part, jnp.zeros((128 - part.shape[0], 128), F32)], axis=0)
                rbuf[v, pl.ds(kg * 16, 16), :] = part.T[:16]
                some = ids[kg * GROUP : (kg + 1) * GROUP]
                some = some + [cands] * (GROUP - len(some))
                gbuf[v, pl.ds(kg * 16, 8), :] = pick([geo_ref[c, 8 * ch : 8 * ch + 8] for c in some])
                gbuf[v, pl.ds(kg * 16 + 8, 8), :] = pick([en_ref[ch, c] for c in some])

    def make_live(e):
        masks = []
        for u in range(GROUP):
            count = len(range(u, neighbours, GROUP))
            part = mask_ref[pl.ds(u * events + e, count, stride=GROUP * events), :].astype(F32)
            part = jnp.concatenate([part, jnp.zeros((PAD_K - count, part.shape[1]), F32)], axis=0)
            masks.append(jnp.concatenate([part, jnp.zeros_like(part)], axis=1))
        for ch in range(CHUNKS):
            for h in range(2):
                parts = []
                for u in range(GROUP):
                    shift = (REP * u - 32 * h - REP * ch) % 128
                    parts.append(pltpu.roll(masks[u], shift, 1) if shift else masks[u])
                live_ref[ch, e, 8 * h : 8 * h + 8] = pick(parts) * (1.0 / all_stations)

    def make_pair(pair, c):
        lanes = lax.broadcasted_iota(jnp.int32, (1, 128), 1)
        slots = jnp.where(lanes < 64, slot_ref[pl.ds(2 * pair, 1), :], slot_ref[pl.ds(2 * pair + 1, 1), :])
        hot_ref[pair] = jnp.where(cand_iota == slots, 1.0, 0.0).astype(BF16)
        for v in range(2):
            make_live(2 * pair + v)
            place = jnp.where(col_e == row_e + (2 * pair + v), -1.0, 0.0).astype(BF16)
            place_ref[pair, 128 * v : 128 * v + 128] = place
        return c

    lax.fori_loop(0, events // 2, make_pair, 0)

    def stage_c(ch, pair, rbuf, gbuf):
        offs_pair, column_pair = [], []
        for v in range(2):
            e = 2 * pair + v

            def quantity(ref, r, v=v):
                return ref[v, pl.ds(r, PAD_K, stride=16), :]

            live = live_ref[ch, e]
            ga = geo_ref[e, 8 * ch : 8 * ch + 8]
            ea = en_ref[ch, e]
            weighted, moved, offs = [], [], [None] * 16
            for h in range(2):
                first = quantity(rbuf, 8 + h)
                first_i = quantity(rbuf, 10 + h)
                alt = quantity(rbuf, 4 + h)
                alt_i = quantity(rbuf, 6 + h)
                power = quantity(rbuf, h) + 64.0 * (first * first - first_i * first_i) - alt * alt
                rough8 = quantity(rbuf, 2 + h) + quantity(rbuf, 14 + h) - 0.125 * (alt_i * alt_i)
                small = 1e-6 * (ea[h : h + 1] * quantity(gbuf, 8 + h) + 1e-6)
                weight = live[8 * h : 8 * h + 8] * power / (power + rough8 + small)
                delayed = weight * quantity(rbuf, 12 + h) / (power + small)
                weighted.append(weight)
                moved.append(delayed)
                gb = [quantity(gbuf, 4 * h + j) for j in range(4)]
                for i in range(4):
                    wi = weight * ga[4 * h + i : 4 * h + i + 1]
                    for j in range(4):
                        term = wi * gb[j]
                        offs[4 * i + j] = term if h == 0 else offs[4 * i + j] + term
            offs_pair.append(jnp.concatenate(offs, axis=0))
            columns = []
            for n, value in enumerate(weighted + moved):
                own_ref[ch, n, pl.ds(e, 1), :] = jnp.sum(value, axis=0, keepdims=True)
                columns.append(
                    jnp.concatenate([jnp.where(block8 == u, value, 0.0) for u in range(GROUP)], axis=0)
                )
            column_pair.append(jnp.concatenate(columns, axis=1))
        offs = jnp.concatenate(offs_pair, axis=1).astype(BF16)
        off_ref[...] += jnp.dot(offs, place_ref[pair], preferred_element_type=F32)
        columns = jnp.concatenate(column_pair, axis=0).astype(BF16)
        acc_ref[ch] += jnp.dot(hot_ref[pair], columns, preferred_element_type=F32)

    for copy in geo_halos:
        copy.wait()

    def spread_got(h, c):
        for i in range(capacity):
            spread_geo(geo_got[h, i], events + h * capacity + i)
        return c

    lax.fori_loop(0, groups_out, spread_got, 0)

    for ch in range(CHUNKS):
        for copy in halos[ch]:
            copy.wait()
        for copy in halos[ch + 1] if ch + 1 < CHUNKS else []:
            copy.start()

        for part in range(imported // GROUP):
            tiles = []
            for n in range(part * GROUP, (part + 1) * GROUP):
                tile = spec_got[ch, n // capacity, n % capacity]
                tiles.append((tile[:REP], tile[REP:]))
            prepare(ch, tiles, events + part * GROUP)

        if ch:
            rbuf_b[...] = jnp.zeros_like(rbuf_b)
        stage_a(ch, 0, cross_a, quad_a)
        pairs = events // 2

        def two_pairs(i, c, ch=ch):
            p = 2 * i
            stage_a(ch, p + 1, cross_b, quad_b)
            stage_b(ch, p, cross_a, quad_a, rbuf_a, gbuf_a)
            stage_c(ch, jnp.maximum(p - 1, 0), rbuf_b, gbuf_b)
            stage_a(ch, jnp.minimum(p + 2, pairs - 1), cross_a, quad_a)
            stage_b(ch, p + 1, cross_b, quad_b, rbuf_b, gbuf_b)
            stage_c(ch, p, rbuf_a, gbuf_a)
            return c

        lax.fori_loop(0, pairs // 2, two_pairs, 0)
        stage_c(ch, pairs - 1, rbuf_b, gbuf_b)

    share = off_ref.shape[0] // sta_n

    def off_copy(d):
        return pltpu.make_async_remote_copy(
            src_ref=off_ref.at[pl.ds(sta_at[d] * share, share)], dst_ref=off_got.at[d - 1],
            send_sem=off_ss.at[d - 1], recv_sem=off_rs.at[d - 1],
            device_id=(sta_at[d], me_c), device_id_type=MESH,
        )

    off_copies = [off_copy(d) for d in range(1, sta_n)]
    for copy in off_copies:
        copy.start()

    lane_out = lax.broadcasted_iota(jnp.int32, (cands, 128), 1)
    pad = jnp.zeros((imported, 128), F32)
    geo_t = geo_ref.reshape(rows * 8 * CHUNKS, 128)
    partial_sums = [None] * 20
    for ch in range(CHUNKS):
        totals = []
        for n in range(4):
            own = jnp.concatenate([own_ref[ch, n], pad], axis=0)
            part = acc_ref[ch, :, n * 128 : (n + 1) * 128]
            totals.append(part + own if n < 2 else own - part)
        geos = [geo_t[pl.ds(8 * ch + n, cands, stride=8 * CHUNKS), :] for n in range(8)]
        for i in range(4):
            scaled = [totals[h] * geos[4 * h + i] for h in range(2)]
            for j in range(i, 5):
                if j < 4:
                    term = scaled[0] * geos[j] + scaled[1] * geos[4 + j]
                else:
                    term = totals[2] * geos[i] + totals[3] * geos[4 + i]
                n = 5 * i + j
                partial_sums[n] = term if ch == 0 else partial_sums[n] + term
    result = jnp.zeros((cands, 128), F32)
    for i in range(4):
        for j in range(i, 5):
            value = jnp.sum(partial_sums[5 * i + j], axis=1, keepdims=True)
            keep = lane_out == 8 * i + j
            if j < 4:
                keep = keep | (lane_out == 8 * j + i)
            result = jnp.where(keep, value, result)
    result = jnp.concatenate([result, jnp.zeros((128 - cands, 128), F32)], axis=0).T
    for x in range(sta_n):
        side_ref[x] = result[8 * x : 8 * x + 8]

    def side_copy(n):
        d, h = peers[n]
        return pltpu.make_async_remote_copy(
            src_ref=side_ref.at[sta_at[d]], dst_ref=side_got.at[n],
            send_sem=side_ss.at[n], recv_sem=side_rs.at[n],
            device_id=(sta_at[d], clu_back[h]), device_id_type=MESH,
        )

    side_copies = [side_copy(n) for n in range(len(peers))]
    for copy in side_copies:
        copy.start()
    for copy in off_copies:
        copy.wait()
    total = off_ref[pl.ds(pl.multiple_of(me_s * share, share), share), :]
    for d in range(1, sta_n):
        total = total + off_got[d - 1]
    for ij in range(share // PAD_K):
        for u in range(GROUP):
            count = len(range(u, neighbours, GROUP))
            block = total[ij * PAD_K : ij * PAD_K + PAD_K, u * 32 : u * 32 + 32]
            last_ref[pl.ds(ij * 128 + 1 + u, count, stride=GROUP), 0:32] = block[:count]
    for copy in side_copies:
        copy.wait()

    kept = side_ref[me_s]
    for n, (d, h) in enumerate(peers):
        if h == groups_out:
            kept = kept + side_got[n]
    away = jnp.zeros((8, 128), F32)
    for h in range(groups_out):
        part = jnp.zeros((8, 128), F32)
        for n, (d, g) in enumerate(peers):
            if g == h:
                part = part + side_got[n]
        lowest = events + h * capacity
        away = jnp.where((lane8 >= lowest) & (lane8 < lowest + capacity), part, away)
    owner_row = jnp.full((1, 128), -1, jnp.int32)
    for h in range(groups_out):
        lowest = events + h * capacity
        inside = (lane8[0:1] >= lowest) & (lane8[0:1] < lowest + capacity)
        owner_row = jnp.where(inside, pltpu.roll(exports_row[h : h + 1, :], lowest, 1), owner_row)
    owner = jnp.where(
        lax.broadcasted_iota(jnp.int32, (events, 128), 0) == owner_row, 1.0, 0.0
    ).astype(BF16)
    back = jnp.zeros((8, events), F32)
    for _ in range(3):
        piece = away.astype(BF16)
        back = back + lax.dot_general(piece, owner, NT, preferred_element_type=F32)
        away = away - piece.astype(F32)
    side = kept[:, :events] + back
    right_out[...] = side[4:5]
    for ij in range(share // PAD_K):
        last_ref[ij * 128 : ij * 128 + 1, 0:32] = side[ij : ij + 1]
        off_out[ij] = last_ref[ij * 128 : ij * 128 + 128, :].T[:events, : neighbours + 1]


def on_device(spectra, partials, pair_list, station_mask, exports):
    events, stations, two_freq = spectra.shape
    sta_n, clu_n = lax.axis_size("sta"), lax.axis_size("clu")
    groups_out, capacity = exports.shape
    half_span = groups_out // 2
    neighbours = pair_list.shape[1]
    imported = groups_out * capacity
    cands = events + imported
    rows = cands + 1
    offsets = [h - half_span + (1 if h >= half_span else 0) for h in range(groups_out)]
    n_peers = sta_n * (groups_out + 1) - 1
    masks = station_mask.transpose(1, 0, 2).reshape(neighbours * events, stations)
    smem = pl.BlockSpec(memory_space=pltpu.SMEM)
    vmem = pl.BlockSpec(memory_space=pltpu.VMEM)
    dma = pltpu.SemaphoreType.DMA
    share = 16 * PAD_K // sta_n
    off, right = pl.pallas_call(
        functools.partial(kernel, offsets, (events, neighbours, sta_n, clu_n, stations * sta_n)),
        out_shape=(
            jax.ShapeDtypeStruct((16 // sta_n, events, neighbours + 1), F32),
            jax.ShapeDtypeStruct((1, events), F32),
        ),
        in_specs=[smem, smem] + [pl.BlockSpec(memory_space=pl.ANY)] * 6,
        out_specs=(vmem, vmem),
        scratch_shapes=[
            pltpu.VMEM(spectra.shape, BF16),
            pltpu.VMEM(partials.shape, BF16),
            pltpu.VMEM(pair_list.shape, jnp.int32),
            pltpu.VMEM(exports.shape, jnp.int32),
            pltpu.VMEM(masks.shape, jnp.int32),
            pltpu.VMEM((2 * two_freq, 5 * two_freq), BF16),
            pltpu.VMEM((8, 128), jnp.int32),
            dma((6,)),
            pltpu.VMEM((CHUNKS, groups_out, capacity, 2 * REP, two_freq), BF16),
            pltpu.VMEM((CHUNKS, groups_out, capacity, 2 * REP, two_freq), BF16),
            pltpu.VMEM((groups_out, capacity, 4, stations), BF16),
            pltpu.VMEM((groups_out, capacity, 4, stations), BF16),
            pltpu.VMEM((CHUNKS, rows, REP, 128), F32),
            pltpu.VMEM((CHUNKS, rows, REP, 128), F32),
            pltpu.VMEM((CHUNKS, rows, REP, 128), F32),
            pltpu.VMEM((CHUNKS, rows, 8, 128), F32),
            pltpu.VMEM((rows, 8 * CHUNKS, 128), F32),
            pltpu.VMEM((events, 128), F32),
            pltpu.VMEM((16 * PAD_K, 256), F32),
            pltpu.VMEM((CHUNKS, cands, 512), F32),
            pltpu.VMEM((CHUNKS, 4, events, 128), F32),
            pltpu.VMEM((sta_n, 8, 128), F32),
            pltpu.VMEM((sta_n - 1, share, 256), F32),
            pltpu.VMEM((n_peers, 8, 128), F32),
            pltpu.VMEM((16 // sta_n * 128, 128), F32),
            pltpu.VMEM((2 * neighbours * REP, 256), BF16),
            pltpu.VMEM((2 * neighbours * REP, 256), BF16),
            pltpu.VMEM((2 * neighbours * REP, 128), BF16),
            pltpu.VMEM((2 * neighbours * REP, 128), BF16),
            pltpu.VMEM((2, PAD_K * 16, 128), F32),
            pltpu.VMEM((2, PAD_K * 16, 128), F32),
            pltpu.VMEM((2, PAD_K * 16, 128), F32),
            pltpu.VMEM((2, PAD_K * 16, 128), F32),
            pltpu.VMEM((CHUNKS, events, 16, 128), F32),
            pltpu.VMEM((events // 2, cands, 128), BF16),
            pltpu.VMEM((events // 2, 256, 256), BF16),
            dma((CHUNKS, groups_out)), dma((CHUNKS, groups_out)), dma((groups_out,)), dma((groups_out,)),
            dma((sta_n - 1,)), dma((sta_n - 1,)), dma((n_peers,)), dma((n_peers,)),
        ],
        compiler_params=pltpu.CompilerParams(
            vmem_limit_bytes=60 << 20, collective_id=0, has_side_effects=True
        ),
    )(
        exports, pair_list, spectra, partials, pair_list, exports, masks,
        jnp.asarray(moment_tables(two_freq // 2)),
    )
    return (off.transpose(0, 2, 1), right)


def solution(mesh):
    return jax.shard_map(
        on_device,
        mesh=mesh,
        in_specs=(
            P("clu", "sta", None),
            P("clu", None, "sta"),
            P("clu", None),
            P("clu", None, "sta"),
            P("clu", None),
        ),
        out_specs=(P("sta", None, "clu"), P("sta", "clu")),
        check_vma=False,
    )
```
